512 devices in a mesh: seq: 32 (over x, z), heads: 2 (over core), dp: 8 (over y).
Axes of the slice: x: 4, y: 8, z: 8, core: 2. Of those that a mesh axis runs over, the one named last changes fastest.
Arguments:
- queries: bfloat16 [32768, 2048], P(('dp', 'seq'), 'heads'), parts along dimension 0, may hold values from -6 to 6
- keys: bfloat16 [32768, 512], P(('dp', 'seq'), 'heads'), parts along dimension 0, may hold values from -6 to 6
- values: bfloat16 [32768, 512], P(('dp', 'seq'), 'heads'), parts along dimension 0, may hold values from -6 to 6
- house: bfloat16 [32768, 512], P(('dp', 'seq'), 'heads'), parts along dimension 0, may hold values from -16 to 16
- beta: float32 [4, 32768], P('heads', ('dp', 'seq')), parts along dimension 1, may hold values from 0.5 to 1.5
- out_weight: bfloat16 [2048, 2048], P('heads'), may hold values from -2 to 2
Outputs:
- mixed: bfloat16 [32768, 2048], P(('dp', 'seq'), 'heads'), parts along dimension 0
The draws below stay inside these ranges and needn't reach their ends.
There are 8 independent parts, one for each index of `dp`. The reference program is written for one: setup_inputs(seed, part) draws one part's arguments, and reference() takes and returns one part's arrays. A program takes and returns all parts, laid end to end along the dimension named above; an argument that names none is the same for every part. Nothing has to cross between parts.
All inputs are finite; a program needn't handle non-finite values.
Results may differ from the reference program's by a relative error of at most 0.012.
Values may be sent and summed in bfloat16 or wider, within the bound.
No kernel may reach another device: no remote copies, remote signals or barrier semaphores. Data moves between devices by JAX's collectives and lax.ppermute only.
A program may use at most 64 MiB of HBM per device.

```python
import math
import jax
import jax.numpy as jnp
from jax import lax

HD = 128
QH = 16
KVH = 4
DW = 2048
TOK_DEV = 128
SEQLEN = 4096


def draw_queries(key, part):
    normal = jax.random.normal(jax.random.fold_in(key, 1), (SEQLEN, QH * HD), jnp.float32)
    rows_out = jnp.clip(normal * 1.5, -6.0, 6.0)
    return rows_out.astype(jnp.bfloat16)


def draw_keys(key, part):
    normal = jax.random.normal(jax.random.fold_in(key, 21), (SEQLEN, KVH * HD), jnp.float32)
    rows_out = jnp.clip(normal, -6.0, 6.0)
    return rows_out.astype(jnp.bfloat16)


def draw_house(key, part):
    blocks = SEQLEN // TOK_DEV
    slow_share = 0.6
    slow_count = max(1, min(HD - 1, int(slow_share * HD)))
    order_keys = jax.random.split(jax.random.fold_in(key, 4), KVH)
    ranks = jax.vmap(lambda one_key: jax.random.permutation(one_key, HD))(order_keys)
    is_slow = ranks < slow_count
    slow_rate = jnp.exp(jax.random.uniform(jax.random.fold_in(key, 8), (KVH, HD), jnp.float32, math.log(1.0 / blocks), math.log(2.0 / blocks)))
    fast_raw = jnp.exp(jax.random.uniform(jax.random.fold_in(key, 9), (KVH, HD), jnp.float32, 0.0, math.log(8.0)))
    slow_sum = jnp.sum(jnp.where(is_slow, slow_rate, 0.0), axis=1, keepdims=True)
    fast_sum = jnp.sum(jnp.where(is_slow, 0.0, fast_raw), axis=1, keepdims=True)
    fast_budget = jnp.maximum(TOK_DEV - slow_sum, 0.5 * TOK_DEV)
    fast_rate = fast_raw * fast_budget / fast_sum
    target = jnp.where(is_slow, slow_rate, fast_rate)
    base_scale = jnp.sqrt(target / jnp.max(target, axis=1, keepdims=True))
    factors = jnp.exp(jax.random.uniform(jax.random.fold_in(key, 5), (blocks, KVH, HD), jnp.float32, -0.35, 0.35))
    noise = jnp.clip(jax.random.normal(jax.random.fold_in(key, 6), (SEQLEN, KVH, HD), jnp.float32), -6.0, 6.0)
    steady = noise * jnp.repeat(factors, TOK_DEV, axis=0) * base_scale[None]
    starts = jax.random.randint(jax.random.fold_in(key, 7), (4,), 0, SEQLEN - 24)
    places = jnp.arange(SEQLEN)
    bursting = jnp.any((places[:, None] >= starts[None, :]) & (places[:, None] < starts[None, :] + 24), axis=1)
    slow_rows = noise * (jnp.min(base_scale, axis=1, keepdims=True) / base_scale)[None]
    rows_out = jnp.where(bursting[:, None, None], slow_rows, steady)
    return rows_out.reshape(SEQLEN, KVH * HD).astype(jnp.bfloat16)


def spiked(values, stream_key, source, target, blocks, factor):
    owner, partner = [(jnp.arange(values.shape[dim]) // (values.shape[dim] // blocks)).reshape([-1 if axis == dim else 1 for axis in range(values.ndim)]) for dim in (source, target)]
    chosen = jax.random.permutation(stream_key, blocks)[partner]
    strong = (owner == chosen) | (owner == (partner + blocks // 2) % blocks)
    return jnp.where(strong, factor * values, values)


def block_levels(rng, dims, pieces, low, top_value):
    loudness = 1.0
    for dim, parts in pieces:
        draws = jax.random.uniform(jax.random.fold_in(jax.random.fold_in(rng, 6), dim), (parts,), jnp.float32, low / len(pieces), top_value / len(pieces))
        loudness = loudness * jnp.repeat(jnp.exp(draws), dims[dim] // parts).reshape((-1,) + (1,) * (len(dims) - 1 - dim))
    return loudness


def gaussian(rng, extent, scale, bound, cuts=(), kind=jnp.bfloat16):
    values = jax.random.normal(rng, extent, jnp.float32) * scale
    if len(cuts) > 0:
        values = block_levels(rng, extent, cuts, -0.22, 0.18) * values
    return jnp.clip(values, min=-bound, max=bound).astype(kind)


def heavy_noise(key, dims, width, most, cuts, heavy, kind=jnp.bfloat16):
    values = width * jax.random.normal(key, dims, jnp.float32)
    if cuts:
        values = values * block_levels(key, dims, cuts, -0.22, 0.18)
    return jnp.clip(spiked(values, jax.random.fold_in(key, 3), *heavy), -most, most).astype(kind)


def setup_inputs(seed: int = 0, part: int = 0) -> dict:
    splits = jax.random.split(jax.random.key(seed), 7)
    own_keys = jax.random.split(jax.random.fold_in(splits[6], part), 7)
    return {
        "queries": draw_queries(jax.random.fold_in(jax.random.fold_in(splits[6], part), 71), part),
        "keys": draw_keys(jax.random.fold_in(jax.random.fold_in(splits[6], part), 71), part),
        "values": gaussian(own_keys[2], (SEQLEN, KVH * HD), 1.0, 6.0, ((0, 32), (1, 2))),
        "house": draw_house(jax.random.fold_in(jax.random.fold_in(splits[6], part), 71), part),
        "beta": jnp.clip(0.5 + 1.0 * jax.random.uniform(own_keys[4], (KVH, SEQLEN), jnp.float32) ** block_levels(own_keys[4], (KVH, SEQLEN), ((0, 2), (1, 32)), -0.2, 0.2), 0.5, 1.5),
        "out_weight": heavy_noise(splits[5], (QH * HD, DW), (HD // 8) ** -0.5, 2.0, ((0, 2),), (0, 1, 2, 2.0)),
    }


highest = lax.Precision.HIGHEST
norm_floor = 1e-06
masked_score = -1e+30

def rounded(values_in):
    return lax.optimization_barrier(values_in.astype(jnp.bfloat16)).astype(jnp.float32)

def unit_vectors(house_rows):
    return house_rows / jnp.sqrt(lax.optimization_barrier(jnp.sum(house_rows * house_rows, axis=-1, keepdims=True)) + norm_floor)

def block_local(query_rows, key_rows, vectors, betas):
    rows_dev, groups, per_group, head_size = query_rows.shape
    start_keys = jnp.zeros((groups, rows_dev, head_size), jnp.float32)
    start_product = jnp.broadcast_to(jnp.eye(head_size, dtype=jnp.float32), (groups, head_size, head_size))

    def token_step(loop_carry, inputs):
        moved_keys, product = loop_carry
        query_row, key_row, vector, beta_row, position = inputs
        along_vector = jnp.einsum('gjd,gd->gj', moved_keys, vector, precision=highest)
        moved_keys = moved_keys - beta_row[:, None, None] * along_vector[:, :, None] * vector[:, None, :]
        moved_keys = lax.dynamic_update_slice(moved_keys, key_row[:, None, :], (jnp.int32(0), position, jnp.int32(0)))
        across = jnp.einsum('gd,gde->ge', vector, product, precision=highest)
        product = product - beta_row[:, None, None] * vector[:, :, None] * across[:, None, :]
        scores = jnp.einsum('gqd,gjd->gqj', query_row, moved_keys, precision=highest)
        turned = jnp.einsum('gab,gqa->gqb', product, query_row, precision=highest)
        return ((moved_keys, product), (scores, turned))
    positions = jnp.arange(rows_dev, dtype=jnp.int32)
    (moved_keys, product), (scores, turned) = lax.scan(token_step, (start_keys, start_product), (query_rows, key_rows, vectors, betas, positions))
    return (scores, turned, moved_keys, product)

def reference(queries, keys, values, house, beta, out_weight):
    groups = KVH
    per_group = QH // KVH
    blocks = SEQLEN // TOK_DEV
    score_scale = 1.0 / math.sqrt(HD)
    query_all = queries.astype(jnp.float32).reshape(blocks, TOK_DEV, groups, per_group, HD)
    key_all = keys.astype(jnp.float32).reshape(blocks, TOK_DEV, groups, HD)
    vector_all = unit_vectors(house.astype(jnp.float32).reshape(blocks, TOK_DEV, groups, HD))
    beta_all = jnp.transpose(beta).reshape(blocks, TOK_DEV, groups)
    value_all = values.astype(jnp.float32).reshape(SEQLEN, groups, HD)
    offsets = jnp.arange(TOK_DEV, dtype=jnp.int32)
    causal = offsets[None, :] <= offsets[:, None]
    columns = jnp.arange(SEQLEN, dtype=jnp.int32)

    def per_block(carried, inputs):
        query_rows, key_rows, vector_rows, beta_rows, block_index = inputs
        scores, turned, moved_keys, product = block_local(query_rows, key_rows, vector_rows, beta_rows)
        start = (block_index * TOK_DEV).astype(jnp.int32)
        local_scores = jnp.where(causal[:, None, None, :], scores * score_scale, masked_score)
        far_scores = jnp.einsum('tgqd,jgd->tgqj', rounded(turned), rounded(carried), precision=highest) * score_scale
        far_scores = jnp.where((columns < start)[None, None, None, :], far_scores, masked_score)
        row_max = jnp.maximum(lax.optimization_barrier(jnp.max(local_scores, axis=-1, keepdims=True)), lax.optimization_barrier(jnp.max(far_scores, axis=-1, keepdims=True)))
        near_weights = jnp.exp(local_scores - row_max)
        far_weights = jnp.exp(far_scores - row_max)
        row_total = lax.optimization_barrier(jnp.sum(near_weights, axis=-1, keepdims=True)) + lax.optimization_barrier(jnp.sum(far_weights, axis=-1, keepdims=True))
        near_values = lax.dynamic_slice_in_dim(value_all, start, TOK_DEV, 0)
        weighted = jnp.einsum('tgqj,jgd->tgqd', rounded(near_weights), near_values, precision=highest)
        weighted = weighted + jnp.einsum('tgqj,jgd->tgqd', rounded(far_weights), value_all, precision=highest)
        attended = (weighted / row_total).astype(jnp.bfloat16).reshape(TOK_DEV, QH * HD)
        block_map = rounded(product)
        carried = jnp.einsum('gba,jga->jgb', block_map, carried, precision=highest)
        block_ends = rounded(jnp.transpose(moved_keys, (1, 0, 2)))
        carried = lax.dynamic_update_slice(carried, block_ends, (start, jnp.int32(0), jnp.int32(0)))
        return (carried, attended)
    start_carry = jnp.zeros((SEQLEN, groups, HD), jnp.float32)
    block_ids = jnp.arange(blocks, dtype=jnp.int32)
    ending, attended = lax.scan(per_block, start_carry, (query_all, key_all, vector_all, beta_all, block_ids))
    attended = attended.reshape(SEQLEN, QH * HD)
    return jnp.dot(attended, out_weight, preferred_element_type=jnp.float32).astype(jnp.bfloat16)
```

```python
import functools
import math

import jax
import jax.numpy as jnp
from jax import lax
from jax.experimental import pallas as pl
from jax.experimental.pallas import tpu as pltpu
from jax.sharding import Mesh, PartitionSpec as P

HD = 128
ROWS = 640
norm_floor = 1e-06
neg = -1e30
qscale = math.log2(math.e) / math.sqrt(HD)
highest = lax.Precision.HIGHEST
f32 = jnp.float32
bf16 = jnp.bfloat16
NN = (((1,), (0,)), ((), ()))
NT = (((1,), (1,)), ((), ()))
TN = (((0,), (0,)), ((), ()))


def dot32(a, b, dims=NN):
    return lax.dot_general(a, b, dims, precision=highest, preferred_element_type=f32)


def dot16(a, b, dims=NN):
    return lax.dot_general(a.astype(bf16), b.astype(bf16), dims, preferred_element_type=f32)


def split(a):
    hi = a.astype(bf16)
    return hi, (a - hi.astype(f32)).astype(bf16)


def unit_inverse(strict):
    row = lax.broadcasted_iota(jnp.int32, (HD, HD), 0)
    col = lax.broadcasted_iota(jnp.int32, (HD, HD), 1)
    eye = (row == col).astype(f32)
    small = jnp.where(row // 8 == col // 8, strict, 0.0)
    square = dot32(small, small)
    fourth = dot32(square, square)
    inv = eye - small
    inv = inv + dot32(inv, square)
    inv = inv + dot32(inv, fourth)
    for size in (8, 16, 32, 64):
        pick = (row // (2 * size) == col // (2 * size)) & (row // size != col // size)
        below = jnp.where(pick, strict, 0.0)
        inv = inv - dot32(inv, dot32(below, inv))
    return inv


def prep_kernel(flag_ref, m0_ref, m1_ref, pay_ref, u_ref, skt_ref, wt_ref, e0_ref, map0t_ref):
    swapped = flag_ref[0] != 0
    row = lax.broadcasted_iota(jnp.int32, (HD, HD), 0)
    col = lax.broadcasted_iota(jnp.int32, (HD, HD), 1)
    eye = (row == col).astype(f32)
    below = col < row
    first = m0_ref[:, 4 * HD :].astype(f32)
    second = m1_ref[:, 4 * HD :].astype(f32)
    blocks = (
        jnp.where(swapped, second, first),
        jnp.where(swapped, first, second),
    )
    maps, ends, turned_values = [], [], []
    for i in range(2):
        block = blocks[i]
        k, v, house = block[:, :HD], block[:, HD : 2 * HD], block[:, 2 * HD : 3 * HD]
        parts = block[:, 3 * HD :]
        beta = parts[:, 0:1] + parts[:, 1:2] + parts[:, 2:3]
        u = house / jnp.sqrt(jnp.sum(house * house, axis=1, keepdims=True) + norm_floor)
        gram = dot32(u, u, NT)
        inv = unit_inverse(jnp.where(below, gram, 0.0) * beta)
        along = jnp.where(below, dot32(u, k, NT), 0.0) * beta
        sk = dot32(inv, along)
        w = dot32(inv, u * beta)
        skt = sk.T
        ends.append(k - dot32(skt, u))
        maps.append(eye - dot32(u, w, TN))
        turned_values.append(v.T)
        u_ref[i] = u
        skt_ref[i] = skt
        wt_ref[i] = w.T
    e0_ref[...] = ends[0].astype(bf16)
    map0t_ref[...] = maps[0].T
    carried = dot32(ends[0], maps[1], NT)
    both = dot32(maps[1], maps[0])
    pieces = (carried, ends[1], turned_values[0], turned_values[1], both)
    for n, piece in enumerate(pieces):
        rounded = piece.astype(bf16)
        for r in range(8):
            pay_ref[r, n * HD : (n + 1) * HD, :] = rounded


def local_kernel(
    flag_ref, m0_ref, m1_ref, u_ref, skt_ref, wt_ref, e0_ref, map0t_ref,
    qt_ref, max_ref, sum_ref, acc_ref,
):
    swapped = flag_ref[0] != 0
    wide = 4 * HD
    key = lax.broadcasted_iota(jnp.int32, (HD, wide), 0)
    token = lax.broadcasted_iota(jnp.int32, (HD, wide), 1) % HD
    upto = key <= token
    first = m0_ref[:, : 6 * HD].astype(f32)
    second = m1_ref[:, : 6 * HD].astype(f32)
    ordered = (
        jnp.where(swapped, second, first),
        jnp.where(swapped, first, second),
    )
    for i in range(2):
        block = ordered[i]
        q = jnp.concatenate([block[:, h * HD : (h + 1) * HD] for h in range(4)], axis=0)
        qt = q.T
        k = block[:, 4 * HD : 5 * HD]
        v = block[:, 5 * HD : 6 * HD]
        uhi, ulo = split(u_ref[i])
        qt16 = qt.astype(bf16)
        qat = jnp.where(upto, dot16(uhi, qt16) + dot16(ulo, qt16), 0.0)
        ahi, alo = split(qat)
        shi, slo = split(skt_ref[i])
        score = dot16(k, qt16) - (dot16(shi, ahi) + dot16(slo, ahi) + dot16(shi, alo))
        score = jnp.where(upto, score * qscale, neg)
        whi, wlo = split(wt_ref[i])
        turned = qt - (dot16(whi, ahi) + dot16(wlo, ahi) + dot16(whi, alo))
        turned = turned * qscale
        values = v.T.astype(bf16)
        if i == 0:
            top = jnp.max(score, axis=0, keepdims=True)
            expo = jnp.exp2(score - top)
            total = jnp.sum(expo, axis=0, keepdims=True)
            acc = dot16(values, expo)
            qt_ref[:, :wide] = turned.astype(bf16)
            values0 = values
        else:
            far = dot16(e0_ref[...], turned)
            top = jnp.maximum(
                jnp.max(score, axis=0, keepdims=True), jnp.max(far, axis=0, keepdims=True)
            )
            expo = jnp.exp2(score - top)
            expo_far = jnp.exp2(far - top)
            total = jnp.sum(expo, axis=0, keepdims=True) + jnp.sum(expo_far, axis=0, keepdims=True)
            acc = dot16(values, expo) + dot16(values0, expo_far)
            thi, tlo = split(turned)
            mhi, mlo = split(map0t_ref[...])
            pulled = dot16(mhi, thi) + dot16(mlo, thi) + dot16(mhi, tlo)
            qt_ref[:, wide:] = pulled.astype(bf16)
        at = i * wide
        max_ref[:, at : at + wide] = top
        sum_ref[:, at : at + wide] = total
        acc_ref[:, at : at + wide] = acc


def far_kernel(
    scalars_ref, own_hbm, other_hbm, qt_ref, max_ref, sum_ref, acc_ref,
    o0_ref, o1_ref, gathered, tops, totals, out, chain, sems,
):
    position = scalars_ref[0]
    core = scalars_ref[1]
    swapped = scalars_ref[2] != 0
    mine = pltpu.make_async_copy(own_hbm, gathered.at[core], sems.at[0])
    theirs = pltpu.make_async_copy(other_hbm, gathered.at[1 - core], sems.at[1])
    mine.start()
    theirs.start()
    tops[...] = max_ref[...]
    totals[...] = sum_ref[...]
    out[...] = acc_ref[...]
    row = lax.broadcasted_iota(jnp.int32, (HD, HD), 0)
    col = lax.broadcasted_iota(jnp.int32, (HD, HD), 1)
    chain[...] = (row == col).astype(f32)
    mine.wait()
    theirs.wait()
    step = 2 * HD

    def visit(n, _):
        source = position - 1 - n
        data = gathered.at[source % 2, source // 2]
        hi, lo = split(chain[...])
        ends = data[: 2 * HD, :]
        keys = (dot16(ends, hi, NT) + dot16(ends, lo, NT)).astype(bf16)
        both = data[4 * HD :, :]
        chain[...] = dot16(hi, both) + dot16(lo, both)
        values = jnp.concatenate([data[2 * HD : 3 * HD, :], data[3 * HD : 4 * HD, :]], axis=1)
        for at in range(0, 8 * HD, step):
            score = dot16(keys, qt_ref[:, at : at + step])
            old = tops[:, at : at + step]
            top = jnp.maximum(old, jnp.max(score, axis=0, keepdims=True))
            shrink = jnp.exp2(old - top)
            expo = jnp.exp2(score - top)
            tops[:, at : at + step] = top
            totals[:, at : at + step] = totals[:, at : at + step] * shrink + jnp.sum(
                expo, axis=0, keepdims=True
            )
            out[:, at : at + step] = out[:, at : at + step] * shrink + dot16(values, expo)
        return 0

    lax.fori_loop(0, position, visit, 0)
    for h in range(4):
        tiles = []
        for i in range(2):
            at = (i * 4 + h) * HD
            tiles.append((out[:, at : at + HD] / totals[:, at : at + HD]).T)
        o0_ref[:, h * HD : (h + 1) * HD] = jnp.where(swapped, tiles[1], tiles[0]).astype(bf16)
        o1_ref[:, h * HD : (h + 1) * HD] = jnp.where(swapped, tiles[0], tiles[1]).astype(bf16)


vmem = pl.BlockSpec(memory_space=pltpu.VMEM)
smem = pl.BlockSpec(memory_space=pltpu.SMEM)
anywhere = pl.BlockSpec(memory_space=pl.ANY)


def shape(dims, kind):
    return jax.ShapeDtypeStruct(dims, kind)


def ways(turn):
    pairs = []
    for z in range(8):
        for core in range(2):
            half, k = z // 4, z % 4
            group = 2 * core + (turn ^ (k % 2))
            pairs.append((z * 2 + core, (2 * group + half) * 2 + k // 2))
    return pairs


def per_device(queries, keys, values, house, beta, out_weight):
    x, m, h, core = (lax.axis_index(a) for a in ("x", "m", "h", "core"))
    ring = ("m", "h", "core")
    wide = 4 * HD
    hi = beta.astype(bf16)
    rest = beta - lax.reduce_precision(beta, 8, 7)
    mid = rest.astype(bf16)
    low = (rest - lax.reduce_precision(rest, 8, 7)).astype(bf16)
    packed_beta = jnp.stack([hi, mid, low], axis=-1)
    packed_beta = jnp.pad(packed_beta, ((0, 0), (0, 0), (0, HD - 3)))

    def message(g):
        return jnp.concatenate(
            [
                queries[:, g * wide : (g + 1) * wide],
                keys[:, g * HD : (g + 1) * HD],
                values[:, g * HD : (g + 1) * HD],
                house[:, g * HD : (g + 1) * HD],
                packed_beta[g],
            ],
            axis=1,
        )

    odd = h == 1
    low_group, high_group = message(0), message(1)
    sent = (jnp.where(odd, high_group, low_group), jnp.where(odd, low_group, high_group))
    got = [lax.ppermute(sent[turn], ring, ways(turn)) for turn in range(2)]
    swapped = (m % 2).astype(jnp.int32)
    flag = swapped.reshape(1)
    payload, u, skt, wt, e0, map0t = pl.pallas_call(
        prep_kernel,
        out_shape=(
            shape((8, ROWS, HD), bf16),
            shape((2, HD, HD), f32),
            shape((2, HD, HD), f32),
            shape((2, HD, HD), f32),
            shape((HD, HD), bf16),
            shape((HD, HD), f32),
        ),
        in_specs=[smem, vmem, vmem],
        out_specs=(vmem,) * 6,
        name="prep",
    )(flag, *got)
    own = lax.all_to_all(payload, ("x", "h"), 0, 0, tiled=True)
    other = lax.ppermute(own, "core", [(0, 1), (1, 0)])
    state = pl.pallas_call(
        local_kernel,
        out_shape=(
            shape((HD, 2 * wide), bf16),
            shape((1, 2 * wide), f32),
            shape((1, 2 * wide), f32),
            shape((HD, 2 * wide), f32),
        ),
        in_specs=[smem] + [vmem] * 7,
        out_specs=(vmem,) * 4,
        name="near",
    )(flag, *got, u, skt, wt, e0, map0t)
    position = 4 * x + 2 * h + core
    scalars = jnp.stack([position, core, swapped]).astype(jnp.int32)
    back = pl.pallas_call(
        far_kernel,
        out_shape=(shape((HD, wide), bf16), shape((HD, wide), bf16)),
        in_specs=[smem, anywhere, anywhere] + [vmem] * 4,
        out_specs=(vmem, vmem),
        scratch_shapes=[
            pltpu.VMEM((2, 8, ROWS, HD), bf16),
            pltpu.VMEM((1, 2 * wide), f32),
            pltpu.VMEM((1, 2 * wide), f32),
            pltpu.VMEM((HD, 2 * wide), f32),
            pltpu.VMEM((HD, HD), f32),
            pltpu.SemaphoreType.DMA((2,)),
        ],
        name="far",
    )(scalars, own, other, *state)
    home = [
        lax.ppermute(back[turn], ring, [(b, a) for a, b in ways(turn)]) for turn in range(2)
    ]
    attended = jnp.concatenate(
        [jnp.where(odd, home[1], home[0]), jnp.where(odd, home[0], home[1])], axis=1
    )
    partial_out = jnp.dot(attended, out_weight, preferred_element_type=f32).astype(bf16)
    halves = jnp.moveaxis(partial_out.reshape(HD, 2, -1), 1, 0)
    arrived = lax.all_to_all(halves, "core", 0, 0, tiled=True)
    return arrived.astype(f32).sum(axis=0).astype(bf16)


def solution(mesh):
    fine = Mesh(mesh.devices.reshape(4, 4, 2, 2, 8), ("x", "m", "h", "core", "dp"))
    rows = ("dp", "x", "m", "h")
    split_rows = P(rows, "core")
    return jax.shard_map(
        per_device,
        mesh=fine,
        in_specs=(split_rows,) * 4 + (P("core", rows), P("core", None)),
        out_specs=split_rows,
        check_vma=False,
    )
```
